256 devices in a mesh: dp: 8 (over x, z_hi), pipe: 4 (over z_lo), expert: 8 (over y, core).
Axes of the slice: x: 4, y: 4, z: 8 (z_hi: 2, z_lo: 4; z = z_hi * 4 + z_lo), core: 2. Of those that a mesh axis runs over, the one named last changes fastest.
Arguments:
- tokens: bfloat16 [8192, 2048], P(('dp', 'expert')), may hold values from -6 to 6
- cotangent: bfloat16 [8192, 2048], P(('dp', 'expert')), may hold values from -6 to 6
- owner_ids: int32 [4, 8192, 4], P('pipe', ('dp', 'expert')), may hold values from 0 to 63, all different within a row; in each aligned block of 32 rows (0 to 31, 32 to 63, ..., all dimensions but the last counted through in order) at most 3 rows name the same one
- gate_weights: bfloat16 [4, 8192, 4], P('pipe', ('dp', 'expert')), may hold values from 0.049804688 to 0.25
- norm_gain: float32 [4, 2048], P('pipe'), may hold values from 0.5 to 1.5
- w_gate: bfloat16 [4, 64, 2048, 384], P('pipe', ('dp', 'expert')), may hold values from -0.125 to 0.125
- w_up: bfloat16 [4, 64, 2048, 384], P('pipe', ('dp', 'expert')), may hold values from -0.125 to 0.125
- w_down: bfloat16 [4, 64, 384, 2048], P('pipe', ('dp', 'expert')), may hold values from -0.3125 to 0.3125
Outputs:
- segment_out: bfloat16 [4, 8192, 2048], P('pipe', ('dp', 'expert'))
- segment_grad: bfloat16 [4, 8192, 2048], P('pipe', ('dp', 'expert'))
- gain_grad: float32 [4, 2048], P('pipe')
The draws below stay inside these ranges and needn't reach their ends.
Inputs may be any that keep to these rules, and one draw needn't show every extreme that they name: `owner_ids`: each row names 4 different owners. In each aligned block of 32 rows (layers in order, then tokens) no owner is named by more than 3 rows, and that bound is reached.
All inputs are finite; a program needn't handle non-finite values.
Results may differ from the reference program's by a relative error of at most 0.014.
Values may be sent and summed in bfloat16 or wider, within the bound.
A program may use at most 128 MiB of HBM per device.

```python
import math
import jax
import jax.numpy as jnp
import numpy as np
from jax import lax

D = 2048
FF = 384
EXP_DEV = 1
ROUTE_OWNERS = 4
MB_ROWS = 32
OWNERS = 64
EXPERTS = 64
CAP = 3
TOKENS = 8192
LAYERS = 4


def levels(rng, extent, cuts, smallest, largest):
    def one(dim, shards_of):
        heights = jax.random.uniform(jax.random.fold_in(jax.random.fold_in(rng, 6), dim), (shards_of,), jnp.float32, smallest / len(cuts), largest / len(cuts))
        return jnp.repeat(jnp.exp(heights), extent[dim] // shards_of).reshape((-1,) + (1,) * (len(extent) - dim - 1))

    loudness = one(*cuts[0])
    for cut in cuts[1:]:
        loudness = loudness * one(*cut)
    return loudness


def routed_block(key, own, number, rows, number_of, top, limit, slope):
    ranking = jax.random.permutation(key, number_of)
    crowded, usual = load_shares(number_of, rows * top, limit, slope, True), load_shares(number_of, rows * top, limit, slope, False)
    places = jnp.arange(number_of)

    def named(sizes, turn):
        used = int((sizes > 0).sum())
        fixed = max(1, used // 4)
        shifted = fixed + (places - fixed + turn * (used - fixed)) % max(1, number_of - fixed)
        return jnp.zeros((number_of,), jnp.int32).at[ranking[jnp.where(places < fixed, places, shifted)]].set(jnp.asarray(sizes, jnp.int32))

    sizes = jnp.where(number % 4 == 0, named(crowded, number // 4), named(usual, number - number // 4 - 1))
    mixed = jax.random.permutation(jax.random.fold_in(own, 3), number_of)
    source_of, receiver = mixed[0:number_of // 2 * 2:2], mixed[1:number_of // 2 * 2:2]
    margin = jnp.minimum(sizes[source_of] - 1, limit - sizes[receiver]) // 2
    margin = jnp.where((source_of == ranking[0]) | (receiver == ranking[0]) | (sizes[receiver] == 0), 0, jnp.maximum(margin, 0))
    shifted = jax.random.randint(jax.random.fold_in(own, 4), (number_of // 2,), 0, 1 << 20) % (margin + 1)
    sizes = sizes.at[source_of].add(-shifted).at[receiver].add(shifted)
    members = jnp.searchsorted(jnp.cumsum(sizes), jnp.arange(rows * top), side="right").astype(jnp.int32)
    listing = members.reshape(top, rows).T
    listing = listing[jax.random.permutation(jax.random.fold_in(own, 1), rows)]
    turn = jax.random.randint(jax.random.fold_in(own, 2), (rows, 1), 0, top)
    return jnp.take_along_axis(listing, (jnp.arange(top)[None, :] + turn) % top, axis=1)


def load_shares(count, total, limit, skew, full):
    weights = [(1 << 20) // math.isqrt(rank ** skew) + 1 for rank in range(1, count + 1)]
    largest = limit if full else min(limit, max(-(-total // count), total * weights[0] // sum(weights)))
    least = 1 if total - largest >= count - 1 else 0
    holding, spare = [largest] + [least] * (count - 1), total - largest - least * (count - 1)
    while spare > 0:
        candidates = [i for i in range(1, count) if holding[i] < largest] or [i for i in range(1, count) if holding[i] < limit]
        mass, left = sum([weights[i] for i in candidates]), spare
        for i in candidates:
            more = min(limit - holding[i], max(1, left * weights[i] // mass), spare)
            holding[i] = holding[i] + more
            spare = spare - more
    return np.array(holding)


def centred(stream_key, extent, spread, reach, pieces=(), kind=jnp.bfloat16):
    result = spread * jax.random.normal(stream_key, extent, jnp.float32)
    if pieces:
        result = result * levels(stream_key, extent, pieces, -0.22, 0.18)
    return jnp.clip(result, -reach, reach).astype(kind)


def setup_inputs(seed: int = 0) -> dict:
    key_of = jax.random.split(jax.random.key(seed), 9)
    tokens = centred(key_of[0], (TOKENS, D), 1.0, 6.0, ((0, 64),))
    cotangent = centred(key_of[1], (TOKENS, D), 1.0, 6.0, ((0, 64),))
    owner_ids_keys = jax.random.split(jax.random.fold_in(key_of[2], 1), LAYERS * TOKENS // MB_ROWS)
    owner_ids_turns = jax.random.permutation(jax.random.fold_in(key_of[2], 3), LAYERS * TOKENS // MB_ROWS)
    owner_ids = jax.vmap(lambda own, number: routed_block(jax.random.fold_in(key_of[2], 2), own, number, MB_ROWS, OWNERS, ROUTE_OWNERS, CAP, 1))(owner_ids_keys, owner_ids_turns).reshape((LAYERS, TOKENS, ROUTE_OWNERS))
    gate_weights = jnp.clip(0.049804688 + 0.20019531 * jax.random.uniform(key_of[3], (LAYERS, TOKENS, EXP_DEV * ROUTE_OWNERS), jnp.float32) ** levels(key_of[3], (LAYERS, TOKENS, EXP_DEV * ROUTE_OWNERS), ((0, 4), (1, 64)), -0.2, 0.2), 0.049804688, 0.25).astype(jnp.bfloat16)
    norm_gain = jnp.clip(1.0 + 0.1 * jax.random.normal(key_of[4], (LAYERS, D), jnp.float32), 0.5, 1.5)
    w_gate = centred(key_of[5], (LAYERS, EXPERTS, D, FF), D ** -0.5, 0.125, ((0, 4), (1, 64)))
    w_up = centred(key_of[6], (LAYERS, EXPERTS, D, FF), D ** -0.5, 0.125, ((0, 4), (1, 64)))
    w_down = centred(key_of[7], (LAYERS, EXPERTS, FF, D), FF ** -0.5, 0.3125, ((0, 4), (1, 64)))
    return dict(tokens=tokens, cotangent=cotangent, owner_ids=owner_ids, gate_weights=gate_weights, norm_gain=norm_gain, w_gate=w_gate, w_up=w_up, w_down=w_down)


epsilon = 1e-06

def inverse_rms(values):
    return lax.rsqrt(lax.optimization_barrier(jnp.mean(values * values, axis=-1, keepdims=True)) + epsilon)

def owner_rows(layer_ids, owner, bound):
    hit_mask = jnp.any(layer_ids == owner, axis=1)
    row_index = jnp.nonzero(hit_mask, size=bound, fill_value=0)[0].astype(jnp.int32)
    hit_count = jnp.sum(hit_mask.astype(jnp.int32))
    is_valid = jnp.arange(bound, dtype=jnp.int32) < hit_count
    chosen = (jnp.take(layer_ids, row_index, axis=0) == owner).astype(jnp.int32)
    which_slot = jnp.argmax(chosen, axis=1).astype(jnp.int32)
    return (row_index, is_valid, which_slot)

def pick_pairs(layer_gates, row_index, which_slot):
    gate_rows = jnp.take(layer_gates, row_index, axis=0)
    columns = (EXP_DEV * which_slot[:, None] + jnp.arange(EXP_DEV, dtype=jnp.int32)[None, :]).astype(jnp.int32)
    return jnp.take_along_axis(gate_rows, columns, axis=1).astype(jnp.float32)

def contract_last(left, right):
    return lax.dot_general(left, right, (((1,), (1,)), ((), ())), preferred_element_type=jnp.float32)

def layer_forward(layer_in, layer_ids, layer_gates, gain_row, gate_mats, up_mats, down_mats):
    x_float = layer_in.astype(jnp.float32)
    scale = inverse_rms(x_float)
    normed = (x_float * scale * gain_row).astype(jnp.bfloat16)
    bound = TOKENS // MB_ROWS * CAP

    def per_owner(branch, owner):
        row_index, is_valid, which_slot = owner_rows(layer_ids, owner, bound)
        picked = jnp.take(normed, row_index, axis=0)
        pairs = pick_pairs(layer_gates, row_index, which_slot)
        summed = jnp.zeros((bound, D), jnp.float32)
        for expert in range(EXP_DEV):
            number = owner * EXP_DEV + expert
            gate_pre = jnp.dot(picked, lax.dynamic_index_in_dim(gate_mats, number, 0, keepdims=False), preferred_element_type=jnp.float32)
            up_pre = jnp.dot(picked, lax.dynamic_index_in_dim(up_mats, number, 0, keepdims=False), preferred_element_type=jnp.float32)
            hidden = (jax.nn.silu(gate_pre) * up_pre).astype(jnp.bfloat16)
            projected = jnp.dot(hidden, lax.dynamic_index_in_dim(down_mats, number, 0, keepdims=False), preferred_element_type=jnp.float32)
            summed = summed + pairs[:, expert:expert + 1] * projected
        rounded = lax.optimization_barrier(summed.astype(jnp.bfloat16)).astype(jnp.float32)
        rounded = jnp.where(is_valid[:, None], rounded, 0.0)
        return (branch.at[row_index].add(rounded), None)
    branch, _ = lax.scan(per_owner, jnp.zeros((TOKENS, D), jnp.float32), jnp.arange(OWNERS, dtype=jnp.int32))
    return (x_float + branch).astype(jnp.bfloat16)

def layer_backward(layer_in, grad_in, layer_ids, layer_gates, gain_row, gate_mats, up_mats, down_mats):
    x_float = layer_in.astype(jnp.float32)
    scale = inverse_rms(x_float)
    normed = (x_float * scale * gain_row).astype(jnp.bfloat16)
    bound = TOKENS // MB_ROWS * CAP

    def per_owner(branch, owner):
        row_index, is_valid, which_slot = owner_rows(layer_ids, owner, bound)
        picked = jnp.take(normed, row_index, axis=0)
        grads = jnp.take(grad_in, row_index, axis=0)
        pairs = pick_pairs(layer_gates, row_index, which_slot)
        summed = jnp.zeros((bound, D), jnp.float32)
        for expert in range(EXP_DEV):
            number = owner * EXP_DEV + expert
            gate_mat = lax.dynamic_index_in_dim(gate_mats, number, 0, keepdims=False)
            up_mat = lax.dynamic_index_in_dim(up_mats, number, 0, keepdims=False)
            down_mat = lax.dynamic_index_in_dim(down_mats, number, 0, keepdims=False)
            gate_pre = jnp.dot(picked, gate_mat, preferred_element_type=jnp.float32)
            up_pre = jnp.dot(picked, up_mat, preferred_element_type=jnp.float32)
            q_vals = contract_last(grads, down_mat)
            sigma = jax.nn.sigmoid(gate_pre)
            weight = pairs[:, expert:expert + 1]
            d_gate = (q_vals * weight * up_pre * sigma * (1.0 + gate_pre * (1.0 - sigma))).astype(jnp.bfloat16)
            d_up = (q_vals * weight * gate_pre * sigma).astype(jnp.bfloat16)
            summed = summed + contract_last(d_gate, gate_mat) + contract_last(d_up, up_mat)
        rounded = lax.optimization_barrier(summed.astype(jnp.bfloat16)).astype(jnp.float32)
        rounded = jnp.where(is_valid[:, None], rounded, 0.0)
        return (branch.at[row_index].add(rounded), None)
    normed_grad, _ = lax.scan(per_owner, jnp.zeros((TOKENS, D), jnp.float32), jnp.arange(OWNERS, dtype=jnp.int32))
    weighted = gain_row * normed_grad
    grad_x = grad_in.astype(jnp.float32) + scale * weighted - x_float * scale * scale * scale * lax.optimization_barrier(jnp.mean(weighted * x_float, axis=-1, keepdims=True))
    gain_part = lax.optimization_barrier(jnp.sum(normed_grad * x_float * scale, axis=0))
    return (grad_x.astype(jnp.bfloat16), gain_part)

def reference(tokens, cotangent, owner_ids, gate_weights, norm_gain, w_gate, w_up, w_down):
    inputs_list = []
    outputs_list = []
    current = tokens
    for layer in range(LAYERS):
        inputs_list.append(current)
        current = layer_forward(current, owner_ids[layer], gate_weights[layer], norm_gain[layer], w_gate[layer], w_up[layer], w_down[layer])
        outputs_list.append(current)
    grads_list = [None] * LAYERS
    gains_list = [None] * LAYERS
    flowing = cotangent
    for layer in range(LAYERS - 1, -1, -1):
        flowing, gain_part = layer_backward(inputs_list[layer], flowing, owner_ids[layer], gate_weights[layer], norm_gain[layer], w_gate[layer], w_up[layer], w_down[layer])
        grads_list[layer] = flowing
        gains_list[layer] = gain_part
    return (jnp.stack(outputs_list), jnp.stack(grads_list), jnp.stack(gains_list))
```

```python
import jax
import jax.numpy as jnp
from jax import lax
from jax.experimental import pallas as pl
from jax.experimental.pallas import tpu as pltpu
from jax.sharding import PartitionSpec as P

MICRO = 4
ROWS = 32
CAP = 3
CHUNKS = 4
EXTRA = 128
EPS = 1e-06
MESH = pl.DeviceIdType.MESH
F32 = jnp.float32
BF16 = jnp.bfloat16


def dot(a, b):
    return jnp.dot(a, b, preferred_element_type=F32)


def dot_last(a, b):
    return lax.dot_general(a, b, (((1,), (1,)), ((), ())), preferred_element_type=F32)


def dot_first(a, b):
    return lax.dot_general(a, b, (((0,), (0,)), ((), ())), preferred_element_type=F32)


def kernel(
    tokens, cotangent, ids, gates, gain, w_gate, w_up, w_down,
    seg_out, seg_grad, gain_out,
    mats, down, cw_own, cw_par, cw_send,
    xa, xb, outs, part, szs, szr, dsend, drec, rsend, rrec, keep, ssq, hid, grad_in, gacc, grec, gtot, gpar,
    s_in_a, s_in_b, s_drec, s_rrec, s_szr, s_dsend, s_rsend, s_szs, s_pga, s_pgb, s_load, s_cw, s_out, s_g,
):
    dp, stage, ex = lax.axis_index("dp"), lax.axis_index("pipe"), lax.axis_index("expert")
    half, xpos = lax.rem(dp, 2), dp // 2
    n_ex = lax.axis_size("expert")
    stages = lax.axis_size("pipe")
    peers = lax.axis_size("dp") * n_ex // 2
    slots = peers * 8
    width = down.shape[1]
    hidden = down.shape[0]
    cw = width // CHUNKS
    me = xpos * n_ex + ex

    def plane(d):
        return (2 * (d // n_ex) + half, stage, lax.rem(d, n_ex))

    partner = (2 * xpos + 1 - half, stage, ex)

    def same(st):
        return (dp, st, ex)

    def other(st):
        return (2 * xpos + 1 - half, st, ex)

    load = [
        pltpu.make_async_copy(w_gate.at[0, 0], mats.at[:, pl.ds(0, hidden)], s_load.at[0]),
        pltpu.make_async_copy(w_up.at[0, 0], mats.at[:, pl.ds(hidden, hidden)], s_load.at[1]),
        pltpu.make_async_copy(w_down.at[0, 0], down, s_load.at[2]),
    ]
    for c in load:
        c.start()

    bar = pltpu.get_barrier_semaphore()

    def greet(dev):
        pl.semaphore_signal(bar, inc=1, device_id=dev, device_id_type=MESH)

    @pl.loop(1, peers)
    def _(i):
        greet(plane(lax.rem(me + i, peers)))

    greet(partner)

    @pl.when(stage > 0)
    def _():
        greet(same(stage - 1))
        greet(other(stage - 1))

    @pl.when(stage < stages - 1)
    def _():
        greet(same(stage + 1))
        greet(other(stage + 1))

    rows = MICRO * ROWS
    n_own = 2 * peers
    lane_o = lax.broadcasted_iota(jnp.int32, (rows, n_own), 1)
    idv = ids[0]
    gv = gates[0].astype(F32)
    member = jnp.zeros((rows, n_own), F32)
    chosen = jnp.zeros((rows, n_own), F32)
    for j in range(idv.shape[1]):
        hit = idv[:, j : j + 1] == lane_o
        member = member + jnp.where(hit, 1.0, 0.0)
        chosen = chosen + jnp.where(hit, gv[:, j : j + 1], 0.0)
    ri = lax.broadcasted_iota(jnp.int32, (rows, rows), 0)
    ci = lax.broadcasted_iota(jnp.int32, (rows, rows), 1)
    earlier = jnp.where((ci < ri) & (ci // ROWS == ri // ROWS), 1.0, 0.0).astype(BF16)
    member = member.astype(BF16)
    position = dot(earlier, member).astype(BF16)
    chosen = chosen.astype(BF16)
    oi = lax.broadcasted_iota(jnp.int32, (n_own, slots), 0)
    si = lax.broadcasted_iota(jnp.int32, (n_own, slots), 1) // 8
    kk = lax.broadcasted_iota(jnp.int32, (rows, slots), 1) % 8

    def table(plane_half, first):
        owner = (2 * (si // n_ex) + plane_half) * n_ex + si % n_ex
        spread = jnp.where(oi == owner, 1.0, 0.0).astype(BF16)
        pos = dot(position, spread)
        wts = dot(chosen, spread)
        return jnp.where(pos == (kk - first).astype(F32), wts, 0.0).astype(BF16)

    cw_own[...] = table(half, 0)
    cw_send[...] = table(1 - half, CAP)
    gacc[...] = jnp.zeros_like(gacc)

    mates = 2 * jnp.where(stage > 0, 1, 0) + 2 * jnp.where(stage < stages - 1, 1, 0)
    pl.semaphore_wait(bar, peers + mates)

    cw_copy = pltpu.make_async_remote_copy(
        cw_send, cw_par, s_cw.at[0], s_cw.at[1], device_id=partner, device_id_type=MESH
    )
    cw_copy.start()

    def cols(k):
        return pl.ds(k * cw, cw)

    def rcols(k, extra):
        if k == 0 and extra:
            return pl.ds(0, EXTRA + cw)
        return pl.ds(EXTRA + k * cw, cw)

    def feed(src, base):
        @pl.loop(0, MICRO)
        def _(m):
            q = base + m
            r = pl.ds(pl.multiple_of(m * ROWS, ROWS), ROWS)
            for k in range(CHUNKS):
                pltpu.make_async_copy(
                    src.at[r, cols(k)], xa.at[q, :, cols(k)], s_in_a.at[q * CHUNKS + k]
                ).start()
                pltpu.make_async_remote_copy(
                    src.at[r, cols(k)], xb.at[q, :, cols(k)], s_g.at[2],
                    s_in_b.at[q * CHUNKS + k], device_id=partner, device_id_type=MESH,
                ).start()

    @pl.when(stage == 0)
    def _():
        feed(tokens, 0)

    for c in load:
        c.wait()
    step = 256

    @pl.loop(0, width // step)
    def _(i):
        r = pl.ds(pl.multiple_of(i * step, step), step)
        mats[r, :] = (mats[r, :].astype(F32) * gain[r, :]).astype(BF16)

    cw_copy.wait()

    def fan_out(send, rec, q, sl, s_send, s_rec):
        pltpu.make_async_copy(send.at[me, pl.ds(0, 2 * CAP), sl], rec.at[q, me, pl.ds(0, 2 * CAP), sl], s_rec).start()

        @pl.loop(1, peers)
        def _(i):
            d = lax.rem(me + i, peers)
            pltpu.make_async_remote_copy(
                send.at[d, pl.ds(0, 2 * CAP), sl], rec.at[q, me, pl.ds(0, 2 * CAP), sl],
                s_send, s_rec, device_id=plane(d), device_id_type=MESH,
            ).start()

    def wait_all(ref, sem):
        pltpu.make_async_copy(ref, ref, sem).wait()

    def section(m, back):
        q = m + (MICRO if back else 0)
        mrow = pl.ds(pl.multiple_of(m * ROWS, ROWS), ROWS)
        both = jnp.concatenate([cw_own[mrow, :], cw_par[mrow, :]], axis=0)
        place = jnp.where(both > 0, 1.0, 0.0).astype(BF16)
        for k in range(CHUNKS):
            i = q * CHUNKS + k
            wait_all(xa.at[q, :, cols(k)], s_in_a.at[i])
            wait_all(xb.at[q, :, cols(k)], s_in_b.at[i])
            src = jnp.concatenate([xa[q, :, cols(k)], xb[q, :, cols(k)]], axis=0)
            dsend[:, :, cols(k)] = dot_first(place, src).astype(BF16).reshape(peers, 8, cw)
            fan_out(dsend, drec, q, cols(k), s_dsend, s_drec.at[i])
        for k in range(CHUNKS):
            i = q * CHUNKS + k
            wait_all(drec.at[q, :, pl.ds(0, 2 * CAP), cols(k)], s_drec.at[i])
            got = drec[q, :, :, cols(k)].reshape(slots, cw)
            if back:
                term = dot_last(got, down[:, cols(k)])
                if k == 0:
                    grad_in[...] = term
                else:
                    grad_in[...] += term
            else:
                term = dot(got, mats[cols(k), :])
                gf = got.astype(F32)
                gf = gf * gf
                sq = gf[:, :128]
                for j in range(1, cw // 128):
                    sq = sq + gf[:, j * 128 : (j + 1) * 128]
                if k == 0:
                    keep[m] = term
                    ssq[...] = sq
                else:
                    keep[m] += term
                    ssq[...] += sq
        if back:
            gp, up = keep[m, :, :hidden], keep[m, :, hidden:]
            qv = grad_in[...]
            sg = jax.nn.sigmoid(gp)
            dg = (qv * up * sg * (1.0 + gp * (1.0 - sg))).astype(BF16)
            du = (qv * gp * sg).astype(BF16)
            hid[:, :hidden] = dg
            hid[:, hidden:] = du
            kap = jnp.sum(dg.astype(F32) * gp + du.astype(F32) * up, axis=1, keepdims=True)
            rsend[:, :, :EXTRA] = jnp.broadcast_to(kap, (slots, EXTRA)).astype(BF16).reshape(peers, 8, EXTRA)
        else:
            scale = lax.rsqrt(jnp.sum(ssq[...], axis=1, keepdims=True) / width + EPS)
            pre = keep[m] * scale
            keep[m] = pre
            gp, up = pre[:, :hidden], pre[:, hidden:]
            hid[:, :hidden] = (gp * jax.nn.sigmoid(gp) * up).astype(BF16)
        for k in range(CHUNKS):
            if back:
                res = dot_last(hid[...], mats[cols(k), :])
            else:
                res = dot(hid[:, :hidden], down[:, cols(k)])
            rsend[:, :, pl.ds(EXTRA + k * cw, cw)] = res.astype(BF16).reshape(peers, 8, cw)
            fan_out(rsend, rrec, q, rcols(k, back), s_rsend, s_rrec.at[q * CHUNKS + k])
        if back:
            xf = xa[m].astype(F32)
            sc = lax.rsqrt(jnp.sum(xf * xf, axis=1, keepdims=True) / width + EPS)
        coef = None
        kap_own = None
        live = lax.broadcasted_iota(jnp.int32, (peers, 8, cw), 1) < 2 * CAP
        for k in range(CHUNKS + 1):
            if k < CHUNKS:
                i = q * CHUNKS + k
                wait_all(rrec.at[q, :, pl.ds(0, 2 * CAP), rcols(k, back)], s_rrec.at[i])
                got = rrec[q, :, :, pl.ds(EXTRA + k * cw, cw)]
                got = jnp.where(live, got, jnp.zeros_like(got)).reshape(slots, cw)
                term = dot(both, got)
                part[:, cols(k)] = term[:ROWS]
                szs[q, :, pl.ds(EXTRA + k * cw, cw)] = term[ROWS:].astype(BF16)
                if back and k == 0:
                    kr = rrec[q, :, :, :EXTRA]
                    kr = jnp.where(live[:, :, :EXTRA], kr, jnp.zeros_like(kr)).reshape(slots, EXTRA)
                    kt = dot(both, kr)
                    kap_own = kt[:ROWS]
                    szs[q, :, :EXTRA] = kt[ROWS:].astype(BF16)
                pltpu.make_async_remote_copy(
                    szs.at[q, :, rcols(k, back)], szr.at[q, :, rcols(k, back)], s_szs,
                    s_szr.at[i], device_id=partner, device_id_type=MESH,
                ).start()
            if k > 0:
                j = k - 1
                i = q * CHUNKS + j
                wait_all(szr.at[q, :, rcols(j, back)], s_szr.at[i])
                add = part[:, cols(j)] + szr[q, :, pl.ds(EXTRA + j * cw, cw)].astype(F32)
                base = xa[q, :, cols(j)].astype(F32)
                if back:
                    if j == 0:
                        kap_all = (kap_own + szr[q, :, :EXTRA].astype(F32))[:, :1]
                        coef = sc * sc * kap_all / width
                    xj = xa[m, :, cols(j)].astype(F32)
                    gacc[:, cols(j)] += jnp.sum(add * xj * sc, axis=0, keepdims=True)
                    res = base + sc * add - xj * coef
                else:
                    res = base + add
                outs[q, :, cols(j)] = res.astype(BF16)

                def pass_on(st):
                    pltpu.make_async_remote_copy(
                        outs.at[q, :, cols(j)], xa.at[q, :, cols(j)], s_pga,
                        s_in_a.at[i], device_id=same(st), device_id_type=MESH,
                    ).start()
                    pltpu.make_async_remote_copy(
                        outs.at[q, :, cols(j)], xb.at[q, :, cols(j)], s_pgb,
                        s_in_b.at[i], device_id=other(st), device_id_type=MESH,
                    ).start()

                if back:

                    @pl.when(stage > 0)
                    def _():
                        pass_on(stage - 1)
                else:

                    @pl.when(stage < stages - 1)
                    def _():
                        pass_on(stage + 1)

        target = seg_grad if back else seg_out
        pltpu.make_async_copy(outs.at[q], target.at[0, mrow, :], s_out.at[q]).start()
        wait_all(dsend.at[pl.ds(0, peers - 1), pl.ds(0, 2 * CAP), :], s_dsend)
        if back:
            wait_all(rsend.at[pl.ds(0, peers - 1), pl.ds(0, 2 * CAP), :], s_rsend)
            wait_all(szs.at[q], s_szs)
        else:
            wait_all(rsend.at[pl.ds(0, peers - 1), pl.ds(0, 2 * CAP), pl.ds(EXTRA, width)], s_rsend)
            wait_all(szs.at[q, :, pl.ds(EXTRA, width)], s_szs)
        passes = (stage > 0) if back else (stage < stages - 1)

        @pl.when(passes)
        def _():
            wait_all(outs.at[q], s_pga)
            wait_all(outs.at[q], s_pgb)

    @pl.loop(0, MICRO)
    def _(m):
        section(m, False)

    @pl.when(stage == stages - 1)
    def _():
        feed(cotangent, MICRO)

    @pl.loop(0, MICRO)
    def _(m):
        section(m, True)

    grec[me] = gacc[...]

    @pl.loop(1, peers)
    def _(i):
        d = lax.rem(me + i, peers)
        pltpu.make_async_remote_copy(
            gacc, grec.at[me], s_g.at[0], s_g.at[1], device_id=plane(d), device_id_type=MESH
        ).start()

    wait_all(grec.at[pl.ds(0, peers - 1)], s_g.at[1])
    wait_all(grec.at[pl.ds(0, peers - 1)], s_g.at[0])
    gtot[...] = jnp.sum(grec[...], axis=0)
    last = pltpu.make_async_remote_copy(
        gtot, gpar, s_g.at[3], s_g.at[4], device_id=partner, device_id_type=MESH
    )
    last.start()
    last.wait()
    gain_out[...] = gtot[...] + gpar[...]

    @pl.when(stage == 0)
    def _():
        wait_all(tokens, s_g.at[2])

    @pl.when(stage == stages - 1)
    def _():
        wait_all(cotangent, s_g.at[2])

    @pl.loop(0, 2 * MICRO)
    def _(q):
        wait_all(outs.at[q], s_out.at[q])


def body(tokens, cotangent, owner_ids, gate_weights, norm_gain, w_gate, w_up, w_down):
    width = tokens.shape[1]
    hidden = w_down.shape[2]
    peers = lax.axis_size("dp") * lax.axis_size("expert") // 2
    slots = peers * 8
    rows = MICRO * ROWS
    wide = EXTRA + width
    gain_col = norm_gain.reshape(width, 1)
    hbm = pl.BlockSpec(memory_space=pl.ANY)
    vmem = pl.BlockSpec(memory_space=pltpu.VMEM)
    dma = pltpu.SemaphoreType.DMA
    seg_out, seg_grad, weighted = pl.pallas_call(
        kernel,
        out_shape=(
            jax.ShapeDtypeStruct((1, rows, width), BF16),
            jax.ShapeDtypeStruct((1, rows, width), BF16),
            jax.ShapeDtypeStruct((1, width), F32),
        ),
        in_specs=[hbm, hbm, vmem, vmem, vmem, hbm, hbm, hbm],
        out_specs=(hbm, hbm, vmem),
        scratch_shapes=[
            pltpu.VMEM((width, 2 * hidden), BF16),
            pltpu.VMEM((hidden, width), BF16),
            pltpu.VMEM((rows, slots), BF16),
            pltpu.VMEM((rows, slots), BF16),
            pltpu.VMEM((rows, slots), BF16),
            pltpu.VMEM((2 * MICRO, ROWS, width), BF16),
            pltpu.VMEM((2 * MICRO, ROWS, width), BF16),
            pltpu.VMEM((2 * MICRO, ROWS, width), BF16),
            pltpu.VMEM((ROWS, width), F32),
            pltpu.VMEM((2 * MICRO, ROWS, wide), BF16),
            pltpu.VMEM((2 * MICRO, ROWS, wide), BF16),
            pltpu.VMEM((peers, 8, width), BF16),
            pltpu.VMEM((2 * MICRO, peers, 8, width), BF16),
            pltpu.VMEM((peers, 8, wide), BF16),
            pltpu.VMEM((2 * MICRO, peers, 8, wide), BF16),
            pltpu.VMEM((MICRO, slots, 2 * hidden), F32),
            pltpu.VMEM((slots, 128), F32),
            pltpu.VMEM((slots, 2 * hidden), BF16),
            pltpu.VMEM((slots, hidden), F32),
            pltpu.VMEM((1, width), F32),
            pltpu.VMEM((peers, 1, width), F32),
            pltpu.VMEM((1, width), F32),
            pltpu.VMEM((1, width), F32),
            dma((2 * MICRO * CHUNKS,)),
            dma((2 * MICRO * CHUNKS,)),
            dma((2 * MICRO * CHUNKS,)),
            dma((2 * MICRO * CHUNKS,)),
            dma((2 * MICRO * CHUNKS,)),
            dma,
            dma,
            dma,
            dma,
            dma,
            dma((3,)),
            dma((2,)),
            dma((2 * MICRO,)),
            dma((5,)),
        ],
        compiler_params=pltpu.CompilerParams(
            collective_id=0, has_side_effects=True, vmem_limit_bytes=56 << 20
        ),
        name="relay",
    )(tokens, cotangent, owner_ids, gate_weights, gain_col, w_gate, w_up, w_down)
    return (seg_out, seg_grad, weighted / norm_gain)


def solution(mesh):
    in_specs = (
        P(("dp", "expert"), None),
        P(("dp", "expert"), None),
        P("pipe", ("dp", "expert"), None),
        P("pipe", ("dp", "expert"), None),
        P("pipe", None),
        P("pipe", ("dp", "expert"), None, None),
        P("pipe", ("dp", "expert"), None, None),
        P("pipe", ("dp", "expert"), None, None),
    )
    out_specs = (
        P("pipe", ("dp", "expert"), None),
        P("pipe", ("dp", "expert"), None),
        P("pipe", None),
    )
    return jax.shard_map(body, mesh=mesh, in_specs=in_specs, out_specs=out_specs, check_vma=False)
```

```python
import jax
import jax.numpy as jnp
from jax import lax
from jax.experimental import pallas as pl
from jax.experimental.pallas import tpu as pltpu
from jax.sharding import PartitionSpec as P

MICRO = 4
ROWS = 32
CAP = 3
WIDTHS = (6, 6, 4)
CHUNKS = len(WIDTHS)
ORDER = "CDDCDC"
EXTRA = 128
EPS = 1e-06
MESH = pl.DeviceIdType.MESH
F32 = jnp.float32
BF16 = jnp.bfloat16


def dot(a, b):
    return jnp.dot(a, b, preferred_element_type=F32)


def dot_last(a, b):
    return lax.dot_general(a, b, (((1,), (1,)), ((), ())), preferred_element_type=F32)


def dot_first(a, b):
    return lax.dot_general(a, b, (((0,), (0,)), ((), ())), preferred_element_type=F32)


def kernel(
    tokens, cotangent, ids, gates, gain, w_gate, w_up, w_down,
    seg_both, gain_out,
    mats, down, cw_own, cw_par, cw_send,
    xa, xb, outs, part, szs, szr, dsend, drec, rsend, rrec, keep, ssq, hid, grad_in, gacc, grec, gtot, gpar,
    s_in_a, s_in_b, s_drec, s_rrec, s_szr, s_dsend, s_rsend, s_szs, s_pga, s_pgb, s_load, s_cw, s_out, s_g,
):
    dp, stage, ex = lax.axis_index("dp"), lax.axis_index("pipe"), lax.axis_index("expert")
    half, xpos = lax.rem(dp, 2), dp // 2
    n_ex = lax.axis_size("expert")
    stages = lax.axis_size("pipe")
    peers = lax.axis_size("dp") * n_ex // 2
    slots = peers * 8
    width = down.shape[1]
    hidden = down.shape[0]
    cws = [w * width // 16 for w in WIDTHS]
    starts = [sum(cws[:k]) for k in range(CHUNKS)]
    me = xpos * n_ex + ex
    ex_at = [lax.rem(ex + i, n_ex) for i in range(n_ex)]

    def plane(d):
        return (2 * (d // n_ex) + half, stage, lax.rem(d, n_ex))

    partner = (2 * xpos + 1 - half, stage, ex)

    def same(st):
        return (dp, st, ex)

    def other(st):
        return (2 * xpos + 1 - half, st, ex)

    load = [
        pltpu.make_async_copy(w_gate.at[0, 0], mats.at[:, pl.ds(0, hidden)], s_load.at[0]),
        pltpu.make_async_copy(w_up.at[0, 0], mats.at[:, pl.ds(hidden, hidden)], s_load.at[1]),
        pltpu.make_async_copy(w_down.at[0, 0], down, s_load.at[2]),
    ]
    for c in load:
        c.start()

    bar = pltpu.get_barrier_semaphore()

    def greet(dev):
        pl.semaphore_signal(bar, inc=1, device_id=dev, device_id_type=MESH)

    @pl.loop(1, peers)
    def _(i):
        greet(plane(lax.rem(me + i, peers)))

    greet(partner)

    @pl.when(stage > 0)
    def _():
        greet(same(stage - 1))
        greet(other(stage - 1))

    @pl.when(stage < stages - 1)
    def _():
        greet(same(stage + 1))
        greet(other(stage + 1))

    rows = MICRO * ROWS
    n_own = 2 * peers
    row_o = lax.broadcasted_iota(jnp.int32, (n_own, rows), 0)
    idv = ids[0]
    gv = gates[0].astype(F32)
    member = jnp.zeros((n_own, rows), F32)
    chosen = jnp.zeros((n_own, rows), F32)
    for j in range(idv.shape[0]):
        hit = idv[j : j + 1, :] == row_o
        member = member + jnp.where(hit, 1.0, 0.0)
        chosen = chosen + jnp.where(hit, gv[j : j + 1, :], 0.0)
    ri = lax.broadcasted_iota(jnp.int32, (rows, rows), 0)
    ci = lax.broadcasted_iota(jnp.int32, (rows, rows), 1)
    earlier = jnp.where((ri < ci) & (ci // ROWS == ri // ROWS), 1.0, 0.0).astype(BF16)
    member = member.astype(BF16)
    position = dot(member, earlier).astype(BF16)
    chosen = chosen.astype(BF16)
    oi = lax.broadcasted_iota(jnp.int32, (n_own, slots), 0)
    si = lax.broadcasted_iota(jnp.int32, (n_own, slots), 1) // 8
    kk = lax.broadcasted_iota(jnp.int32, (rows, slots), 1) % 8

    def table(plane_half, first):
        owner = (2 * (si // n_ex) + plane_half) * n_ex + si % n_ex
        spread = jnp.where(oi == owner, 1.0, 0.0).astype(BF16)
        pos = dot_first(position, spread)
        wts = dot_first(chosen, spread)
        return jnp.where(pos == (kk - first).astype(F32), wts, 0.0).astype(BF16)

    cw_own[...] = table(half, 0)
    cw_send[...] = table(1 - half, CAP)
    gacc[...] = jnp.zeros_like(gacc)

    mates = 2 * jnp.where(stage > 0, 1, 0) + 2 * jnp.where(stage < stages - 1, 1, 0)
    pl.semaphore_wait(bar, peers + mates)

    cw_copy = pltpu.make_async_remote_copy(
        cw_send, cw_par, s_cw.at[0], s_cw.at[1], device_id=partner, device_id_type=MESH
    )
    cw_copy.start()

    def cols(k):
        return pl.ds(starts[k], cws[k])

    def rdata(k):
        return pl.ds(EXTRA + starts[k], cws[k])

    def rcols(k, extra):
        if k == 0 and extra:
            return pl.ds(0, EXTRA + cws[0])
        return rdata(k)

    def feed(src, base):
        @pl.loop(0, MICRO)
        def _(m):
            q = base + m
            r = pl.ds(pl.multiple_of(m * ROWS, ROWS), ROWS)
            for k in range(CHUNKS):
                pltpu.make_async_copy(
                    src.at[r, cols(k)], xa.at[q, :, cols(k)], s_in_a.at[q * CHUNKS + k]
                ).start()
                pltpu.make_async_remote_copy(
                    src.at[r, cols(k)], xb.at[q, :, cols(k)], s_g.at[2],
                    s_in_b.at[q * CHUNKS + k], device_id=partner, device_id_type=MESH,
                ).start()

    @pl.when(stage == 0)
    def _():
        feed(tokens, 0)

    cw_copy.wait()

    def fan_out(send, rec, q, sl, s_send, s_rec):
        pltpu.make_async_copy(send.at[me, pl.ds(0, 2 * CAP), sl], rec.at[q, me, pl.ds(0, 2 * CAP), sl], s_rec).start()

        def to_row(dx, first):
            x = lax.rem(xpos + dx, peers // n_ex)
            for de in range(first, n_ex):
                e = ex_at[de]
                d = x * n_ex + e
                pltpu.make_async_remote_copy(
                    send.at[d, pl.ds(0, 2 * CAP), sl], rec.at[q, me, pl.ds(0, 2 * CAP), sl],
                    s_send, s_rec, device_id=(2 * x + half, stage, e), device_id_type=MESH,
                ).start()

        to_row(0, 1)

        @pl.loop(1, peers // n_ex)
        def _(dx):
            to_row(dx, 0)

    def wait_all(ref, sem):
        pltpu.make_async_copy(ref, ref, sem).wait()

    def tables(m):
        mrow = pl.ds(pl.multiple_of(m * ROWS, ROWS), ROWS)
        return jnp.concatenate([cw_own[mrow, :], cw_par[mrow, :]], axis=0)

    def dispatch(m, back, prior):
        q = m + (MICRO if back else 0)
        place = jnp.where(tables(m) > 0, 1.0, 0.0).astype(BF16)
        for k in range(CHUNKS):
            i = q * CHUNKS + k
            wait_all(xa.at[q, :, cols(k)], s_in_a.at[i])
            wait_all(xb.at[q, :, cols(k)], s_in_b.at[i])
            if k == 0 and prior:
                wait_all(dsend.at[pl.ds(0, peers - 1), pl.ds(0, 2 * CAP), :], s_dsend)
            src = jnp.concatenate([xa[q, :, cols(k)], xb[q, :, cols(k)]], axis=0)
            dsend[:, :, cols(k)] = dot_first(place, src).astype(BF16).reshape(peers, 8, cws[k])
            fan_out(dsend, drec, q, cols(k), s_dsend, s_drec.at[i])
            yield

    def sent_back(back):
        if back:
            wait_all(rsend.at[pl.ds(0, peers - 1), pl.ds(0, 2 * CAP), :], s_rsend)
        else:
            wait_all(rsend.at[pl.ds(0, peers - 1), pl.ds(0, 2 * CAP), pl.ds(EXTRA, width)], s_rsend)

    def expert(m, back, prior):
        q = m + (MICRO if back else 0)
        for k in range(CHUNKS):
            i = q * CHUNKS + k
            wait_all(drec.at[q, :, pl.ds(0, 2 * CAP), cols(k)], s_drec.at[i])
            got = drec[q, :, :, cols(k)].reshape(slots, cws[k])
            if back:
                term = dot_last(got, down[:, cols(k)])
                if k == 0:
                    grad_in[...] = term
                else:
                    grad_in[...] += term
            else:
                term = dot(got, mats[cols(k), :])
                gf = got.astype(F32)
                gf = gf * gf
                sq = gf[:, :128]
                for j in range(1, cws[k] // 128):
                    sq = sq + gf[:, j * 128 : (j + 1) * 128]
                if k == 0:
                    keep[m] = term
                    ssq[...] = sq
                else:
                    keep[m] += term
                    ssq[...] += sq
        if prior is not None:
            sent_back(prior)
        if back:
            gp, up = keep[m, :, :hidden], keep[m, :, hidden:]
            qv = grad_in[...]
            sg = jax.nn.sigmoid(gp)
            dg = (qv * up * sg * (1.0 + gp * (1.0 - sg))).astype(BF16)
            du = (qv * gp * sg).astype(BF16)
            hid[:, :hidden] = dg
            hid[:, hidden:] = du
            kap = jnp.sum(dg.astype(F32) * gp + du.astype(F32) * up, axis=1, keepdims=True)
            rsend[:, :, :EXTRA] = jnp.broadcast_to(kap, (slots, EXTRA)).astype(BF16).reshape(peers, 8, EXTRA)
        else:
            scale = lax.rsqrt(jnp.sum(ssq[...], axis=1, keepdims=True) / width + EPS)
            pre = keep[m] * scale
            keep[m] = pre
            gp, up = pre[:, :hidden], pre[:, hidden:]
            hid[:, :hidden] = (gp * jax.nn.sigmoid(gp) * up).astype(BF16)
        for k in range(CHUNKS):
            if back:
                res = dot_last(hid[...], mats[cols(k), :])
            else:
                res = dot(hid[:, :hidden], down[:, cols(k)])
            rsend[:, :, rdata(k)] = res.astype(BF16).reshape(peers, 8, cws[k])
            fan_out(rsend, rrec, q, rcols(k, back), s_rsend, s_rrec.at[q * CHUNKS + k])

    def collect(m, back):
        q = m + (MICRO if back else 0)
        both = tables(m)
        if back:
            xf = xa[m].astype(F32)
            sc = lax.rsqrt(jnp.sum(xf * xf, axis=1, keepdims=True) / width + EPS)
        coef = None
        kap_own = None

        def summed(sl, n):
            got = rrec[q, :, :, sl]
            live = lax.broadcasted_iota(jnp.int32, (peers, 8, n), 1) < 2 * CAP
            got = jnp.where(live, got, jnp.zeros_like(got)).reshape(slots, n)
            return dot(both, got)

        for k in range(CHUNKS + 1):
            if k < CHUNKS:
                i = q * CHUNKS + k
                wait_all(rrec.at[q, :, pl.ds(0, 2 * CAP), rcols(k, back)], s_rrec.at[i])
                term = summed(rdata(k), cws[k])
                part[:, cols(k)] = term[:ROWS]
                szs[q, :, rdata(k)] = term[ROWS:].astype(BF16)
                if back and k == 0:
                    kt = summed(pl.ds(0, EXTRA), EXTRA)
                    kap_own = kt[:ROWS]
                    szs[q, :, :EXTRA] = kt[ROWS:].astype(BF16)
                pltpu.make_async_remote_copy(
                    szs.at[q, :, rcols(k, back)], szr.at[q, :, rcols(k, back)], s_szs.at[q],
                    s_szr.at[i], device_id=partner, device_id_type=MESH,
                ).start()
            if k > 0:
                j = k - 1
                i = q * CHUNKS + j
                wait_all(szr.at[q, :, rcols(j, back)], s_szr.at[i])
                add = part[:, cols(j)] + szr[q, :, rdata(j)].astype(F32)
                base = xa[q, :, cols(j)].astype(F32)
                if back:
                    if j == 0:
                        kap_all = (kap_own + szr[q, :, :EXTRA].astype(F32))[:, :1]
                        coef = sc * sc * kap_all / width
                    xj = xa[m, :, cols(j)].astype(F32)
                    gacc[:, cols(j)] += jnp.sum(add * xj * sc, axis=0, keepdims=True)
                    res = base + sc * add - xj * coef
                else:
                    res = base + add
                outs[q, :, cols(j)] = res.astype(BF16)

                def pass_on(st):
                    pltpu.make_async_remote_copy(
                        outs.at[q, :, cols(j)], xb.at[q, :, cols(j)], s_pgb.at[q],
                        s_in_b.at[i], device_id=other(st), device_id_type=MESH,
                    ).start()
                    pltpu.make_async_remote_copy(
                        outs.at[q, :, cols(j)], xa.at[q, :, cols(j)], s_pga.at[q],
                        s_in_a.at[i], device_id=same(st), device_id_type=MESH,
                    ).start()

                if back:

                    @pl.when(stage > 0)
                    def _():
                        pass_on(stage - 1)
                else:

                    @pl.when(stage < stages - 1)
                    def _():
                        pass_on(stage + 1)

            if k < CHUNKS:
                yield
        mrow = pl.ds(pl.multiple_of(m * ROWS, ROWS), ROWS)
        pltpu.make_async_copy(outs.at[q], seg_both.at[int(back), mrow, :], s_out.at[q]).start()

    def run(first, second=None, order=ORDER):
        if second is not None:
            for c in order:
                next(first if c == "C" else second, None)
        for g in (first, second):
            if g is not None:
                for _ in g:
                    pass

    run(dispatch(0, False, False))
    for c in load:
        c.wait()
    eye_r = lax.broadcasted_iota(jnp.int32, (128, 128), 0)
    eye_c = lax.broadcasted_iota(jnp.int32, (128, 128), 1)

    @pl.loop(0, width // 128)
    def _(i):
        r = pl.ds(pl.multiple_of(i * 128, 128), 128)
        col = jnp.sum(jnp.where(eye_r == eye_c, gain[:, r], 0.0), axis=1, keepdims=True)
        mats[r, :] = (mats[r, :].astype(F32) * col).astype(BF16)

    expert(0, False, None)

    @pl.loop(0, MICRO - 1)
    def _(m):
        run(collect(m, False), dispatch(m + 1, False, True))
        expert(m + 1, False, False)

    @pl.when(stage == stages - 1)
    def _():
        feed(cotangent, MICRO)
        run(dispatch(0, True, True))

    run(collect(MICRO - 1, False))

    @pl.when(stage < stages - 1)
    def _():
        run(dispatch(0, True, True))

    expert(0, True, False)

    @pl.loop(0, MICRO - 1)
    def _(m):
        run(collect(m, True), dispatch(m + 1, True, True))
        expert(m + 1, True, True)

    run(collect(MICRO - 1, True))
    wait_all(dsend.at[pl.ds(0, peers - 1), pl.ds(0, 2 * CAP), :], s_dsend)
    sent_back(True)

    grec[me] = gacc[...]

    @pl.loop(1, peers)
    def _(i):
        d = lax.rem(me + i, peers)
        pltpu.make_async_remote_copy(
            gacc, grec.at[me], s_g.at[0], s_g.at[1], device_id=plane(d), device_id_type=MESH
        ).start()

    wait_all(grec.at[pl.ds(0, peers - 1)], s_g.at[1])
    wait_all(grec.at[pl.ds(0, peers - 1)], s_g.at[0])
    gtot[...] = jnp.sum(grec[...], axis=0)
    last = pltpu.make_async_remote_copy(
        gtot, gpar, s_g.at[3], s_g.at[4], device_id=partner, device_id_type=MESH
    )
    last.start()
    last.wait()
    gain_out[...] = gtot[...] + gpar[...]

    @pl.when(stage == 0)
    def _():
        wait_all(tokens, s_g.at[2])

    @pl.when(stage == stages - 1)
    def _():
        wait_all(cotangent, s_g.at[2])

    def left(q, sl, passes):
        wait_all(outs.at[q], s_out.at[q])
        wait_all(szs.at[q, :, sl], s_szs.at[q])

        @pl.when(passes)
        def _():
            wait_all(outs.at[q], s_pga.at[q])
            wait_all(outs.at[q], s_pgb.at[q])

    @pl.loop(0, MICRO)
    def _(m):
        left(m, pl.ds(EXTRA, width), stage < stages - 1)
        left(m + MICRO, pl.ds(0, EXTRA + width), stage > 0)


def body(tokens, cotangent, owner_ids, gate_weights, norm_gain, w_gate, w_up, w_down):
    width = tokens.shape[1]
    hidden = w_down.shape[2]
    peers = lax.axis_size("dp") * lax.axis_size("expert") // 2
    slots = peers * 8
    rows = MICRO * ROWS
    wide = EXTRA + width
    ids = jnp.swapaxes(owner_ids, 1, 2)
    gates = jnp.swapaxes(gate_weights, 1, 2)
    hbm = pl.BlockSpec(memory_space=pl.ANY)
    vmem = pl.BlockSpec(memory_space=pltpu.VMEM)
    dma = pltpu.SemaphoreType.DMA
    both, weighted = pl.pallas_call(
        kernel,
        out_shape=(
            jax.ShapeDtypeStruct((2, rows, width), BF16),
            jax.ShapeDtypeStruct((1, width), F32),
        ),
        in_specs=[hbm, hbm, vmem, vmem, vmem, hbm, hbm, hbm],
        out_specs=(hbm, vmem),
        scratch_shapes=[
            pltpu.VMEM((width, 2 * hidden), BF16),
            pltpu.VMEM((hidden, width), BF16),
            pltpu.VMEM((rows, slots), BF16),
            pltpu.VMEM((rows, slots), BF16),
            pltpu.VMEM((rows, slots), BF16),
            pltpu.VMEM((2 * MICRO, ROWS, width), BF16),
            pltpu.VMEM((2 * MICRO, ROWS, width), BF16),
            pltpu.VMEM((2 * MICRO, ROWS, width), BF16),
            pltpu.VMEM((ROWS, width), F32),
            pltpu.VMEM((2 * MICRO, ROWS, wide), BF16),
            pltpu.VMEM((2 * MICRO, ROWS, wide), BF16),
            pltpu.VMEM((peers, 8, width), BF16),
            pltpu.VMEM((2 * MICRO, peers, 8, width), BF16),
            pltpu.VMEM((peers, 8, wide), BF16),
            pltpu.VMEM((2 * MICRO, peers, 8, wide), BF16),
            pltpu.VMEM((MICRO, slots, 2 * hidden), F32),
            pltpu.VMEM((slots, 128), F32),
            pltpu.VMEM((slots, 2 * hidden), BF16),
            pltpu.VMEM((slots, hidden), F32),
            pltpu.VMEM((1, width), F32),
            pltpu.VMEM((peers, 1, width), F32),
            pltpu.VMEM((1, width), F32),
            pltpu.VMEM((1, width), F32),
            dma((2 * MICRO * CHUNKS,)),
            dma((2 * MICRO * CHUNKS,)),
            dma((2 * MICRO * CHUNKS,)),
            dma((2 * MICRO * CHUNKS,)),
            dma((2 * MICRO * CHUNKS,)),
            dma,
            dma,
            dma((2 * MICRO,)),
            dma((2 * MICRO,)),
            dma((2 * MICRO,)),
            dma((3,)),
            dma((2,)),
            dma((2 * MICRO,)),
            dma((5,)),
        ],
        compiler_params=pltpu.CompilerParams(
            collective_id=0, has_side_effects=True, vmem_limit_bytes=56 << 20
        ),
        name="relay",
    )(tokens, cotangent, ids, gates, norm_gain, w_gate, w_up, w_down)
    return (both[0:1], both[1:2], weighted / norm_gain)


def solution(mesh):
    in_specs = (
        P(("dp", "expert"), None),
        P(("dp", "expert"), None),
        P("pipe", ("dp", "expert"), None),
        P("pipe", ("dp", "expert"), None),
        P("pipe", None),
        P("pipe", ("dp", "expert"), None, None),
        P("pipe", ("dp", "expert"), None, None),
        P("pipe", ("dp", "expert"), None, None),
    )
    out_specs = (
        P("pipe", ("dp", "expert"), None),
        P("pipe", ("dp", "expert"), None),
        P("pipe", None),
    )
    return jax.shard_map(body, mesh=mesh, in_specs=in_specs, out_specs=out_specs, check_vma=False)
```
